512 devices in a mesh: uly: 8 (over y_hi, core), blk: 64 (over z, x, y_lo).
Axes of the slice: x: 4, y: 8 (y_hi: 4, y_lo: 2; y = y_hi * 2 + y_lo), z: 8, core: 2. Of those that a mesh axis runs over, the one named last changes fastest.
Arguments:
- query_proj: bfloat16 [192, 384, 3072], P('blk', 'uly'), may hold values from -16 to 16
- key_proj: bfloat16 [192, 384, 3072], P('blk', 'uly'), may hold values from -16 to 16
- value_proj: bfloat16 [192, 384, 3072], P('blk', 'uly'), may hold values from -6 to 6
- query_gain: float32 [128], replicated, may hold values from 0.5 to 8
- key_gain: float32 [128], replicated, may hold values from 0.5 to 8
- neighbours: int32 [192, 9], P('blk'), may hold values from 0 to 191, as said below
- tile_counts: int32 [192], P('blk'), may hold values from 1 to 9, as said below
Outputs:
- attention: bfloat16 [192, 384, 3072], P('blk', 'uly')
The draws below stay inside these ranges and needn't reach their ends.
Inputs may be any that keep to these rules, and one draw needn't show every extreme that they name: `neighbours`: the first tile_counts[t] entries of row t are distinct tiles; entry 0 is t itself; every entry lies in the slab of tile t or in one of the two slabs beside it, a slab being the tiles with equal index // 3; entries at positions tile_counts[t] and beyond equal t. `tile_counts`: some tile lists 9 tiles.
All inputs are finite; a program needn't handle non-finite values.
Results may differ from the reference program's by a relative error of at most 0.005.
The reference program's roundings to bfloat16 on the way (of `query_norm`, `key_norm` and `rounded`) count: a program that leaves them out, or rounds other values in their place, can miss the bound.
Values may be sent and summed in bfloat16 or wider, within the bound.
No kernel may reach another device: no remote copies, remote signals or barrier semaphores. Data moves between devices by JAX's collectives and lax.ppermute only.
A program may use at most 128 MiB of HBM per device.

```python
import jax
import jax.numpy as jnp
from jax import lax

HEADS = 24
HD = 128
TILE = 384
NBMAX = 9
TILES_DEV = 3
TILES = 192


def draw_gain(key):
    spread = jax.random.uniform(key, (HD,))
    gains = 0.5 + spread
    return gains.astype(jnp.float32)


def draw_query_gain(key, part):
    return draw_gain(jax.random.fold_in(key, 21))


def draw_key_gain(key, part):
    return draw_gain(jax.random.fold_in(key, 22))


def draw_query_proj(key, part):
    noise = jax.random.normal(jax.random.fold_in(key, 1), (TILES, TILE, HEADS * HD))
    return jnp.clip(noise, -16.0, 16.0).astype(jnp.bfloat16)


def draw_key_proj(key, part):
    noise = jax.random.normal(jax.random.fold_in(key, 2), (TILES, TILE, HEADS * HD))
    return jnp.clip(noise, -16.0, 16.0).astype(jnp.bfloat16)


def count_table(key):
    slab_count = TILES // TILES_DEV
    tile_idx = jnp.arange(TILES, dtype=jnp.int32)
    slab = tile_idx // TILES_DEV
    lowest = jax.random.randint(jax.random.fold_in(key, 1), (slab_count,), max(NBMAX - 5, 1), NBMAX + 1)
    counts = jax.random.randint(jax.random.fold_in(key, 2), (TILES,), lowest[slab], NBMAX + 1)
    edge = (slab == 0) | (slab == slab_count - 1)
    counts = jnp.where(edge, jnp.minimum(counts, 2 * TILES_DEV), counts)
    chosen = jax.random.randint(jax.random.fold_in(key, 3), (), TILES_DEV, TILES - TILES_DEV)
    return jnp.where(tile_idx == chosen, NBMAX, counts).astype(jnp.int32)


def draw_tile_counts(key, part):
    return count_table(jax.random.fold_in(key, 11))


def draw_neighbours(key, part):
    counts = count_table(jax.random.fold_in(key, 11))
    span = 3 * TILES_DEV
    tile_idx = jnp.arange(TILES, dtype=jnp.int32)
    slab = tile_idx // TILES_DEV
    candidates = (slab[:, None] - 1) * TILES_DEV + jnp.arange(span, dtype=jnp.int32)[None, :]
    usable = (candidates >= 0) & (candidates < TILES) & (candidates != tile_idx[:, None])
    row_keys = jax.random.split(jax.random.fold_in(key, 12), TILES)
    priority = jax.vmap(lambda row_key: jax.random.permutation(row_key, span))(row_keys).astype(jnp.int32)
    sort_keys = jnp.where(usable, priority, priority + span)
    order = jnp.argsort(sort_keys, axis=1)
    picked = jnp.take_along_axis(candidates, order, axis=1)[:, :NBMAX - 1]
    listed = jnp.concatenate([tile_idx[:, None], picked], axis=1)
    position = jnp.arange(NBMAX, dtype=jnp.int32)[None, :]
    return jnp.where(position < counts[:, None], listed, tile_idx[:, None]).astype(jnp.int32)


def block_levels(stream_key, dims, pieces, least, top_value):
    factor_of = 1.0
    for dim, parts in pieces:
        steps = jax.random.uniform(jax.random.fold_in(jax.random.fold_in(stream_key, 6), dim), (parts,), jnp.float32, least / len(pieces), top_value / len(pieces))
        factor_of = factor_of * jnp.repeat(jnp.exp(steps), dims[dim] // parts).reshape((-1,) + (1,) * (len(dims) - 1 - dim))
    return factor_of


def normal_values(key, shape, scale, reach, cuts=(), kind=jnp.bfloat16):
    loudness = block_levels(key, shape, cuts, -0.22, 0.18) if cuts else 1.0
    result = jax.random.normal(key, shape, jnp.float32) * scale * loudness
    return jnp.minimum(jnp.maximum(result, -reach), reach).astype(kind)


def setup_inputs(seed: int = 0) -> dict:
    seeds = jax.random.split(jax.random.key(seed), 8)
    query_proj = draw_query_proj(jax.random.fold_in(seeds[7], 71), 0)
    key_proj = draw_key_proj(jax.random.fold_in(seeds[7], 71), 0)
    value_proj = normal_values(seeds[2], (TILES, TILE, HEADS * HD), 1.0, 6.0, ((0, 64), (1, 8)))
    query_gain = draw_query_gain(jax.random.fold_in(seeds[7], 71), 0)
    key_gain = draw_key_gain(jax.random.fold_in(seeds[7], 71), 0)
    neighbours = draw_neighbours(jax.random.fold_in(seeds[7], 71), 0)
    tile_counts = draw_tile_counts(jax.random.fold_in(seeds[7], 71), 0)
    return {"query_proj": query_proj, "key_proj": key_proj, "value_proj": value_proj, "query_gain": query_gain, "key_gain": key_gain, "neighbours": neighbours, "tile_counts": tile_counts}


def normalize_heads(values_in, gain_vec):
    widened = values_in.astype(jnp.float32)
    widened = widened.reshape(widened.shape[:-1] + (widened.shape[-1] // HD, HD))
    scaled = widened * lax.rsqrt(lax.optimization_barrier(jnp.mean(widened * widened, axis=-1, keepdims=True)) + 1e-06) * gain_vec
    return scaled.astype(jnp.bfloat16).reshape(values_in.shape)

def attend_tile(query_tile, key_tiles, value_tiles, live_count):
    head_count = query_tile.shape[-1] // HD
    rows = query_tile.shape[0]
    inv_root = HD ** (-0.5)
    query_rows = query_tile.reshape(rows, head_count, HD).astype(jnp.float32)
    key_rows = key_tiles.reshape(-1, head_count, HD).astype(jnp.float32)
    value_rows = value_tiles.reshape(-1, head_count, HD).astype(jnp.float32)
    scores = jnp.einsum('qhd,khd->hqk', query_rows, key_rows) * inv_root
    live_keys = jnp.repeat(jnp.arange(key_tiles.shape[0], dtype=jnp.int32) < live_count, key_tiles.shape[1])
    scores = jnp.where(live_keys, scores, jnp.float32(-1e+30))
    row_max = lax.optimization_barrier(jnp.max(scores, axis=-1, keepdims=True))
    weights = jnp.where(live_keys, jnp.exp(scores - row_max), jnp.float32(0.0))
    totals = lax.optimization_barrier(jnp.sum(weights, axis=-1))
    rounded = weights.astype(jnp.bfloat16)
    numerator = jnp.einsum('hqk,khd->qhd', rounded.astype(jnp.float32), value_rows)
    attended = numerator / jnp.transpose(totals)[:, :, None]
    return attended.astype(jnp.bfloat16).reshape(rows, head_count * HD)

def reference(query_proj, key_proj, value_proj, query_gain, key_gain, neighbours, tile_counts):
    query_norm = normalize_heads(query_proj, query_gain)
    key_norm = normalize_heads(key_proj, key_gain)

    def attend(tile_idx):
        slots = neighbours[tile_idx]
        return attend_tile(query_norm[tile_idx], key_norm[slots], value_proj[slots], tile_counts[tile_idx])
    return lax.map(attend, jnp.arange(TILES, dtype=jnp.int32))
```

```python
import functools
import math

import jax
import jax.numpy as jnp
import numpy as np
from jax import lax
from jax.experimental import pallas as pl
from jax.experimental.pallas import tpu as pltpu
from jax.sharding import Mesh
from jax.sharding import PartitionSpec as P

HD = 128
NB = 9
TD = 3
LOC = 48
COLS = 8 * 4
SIZES = (4, 2, 8, 4, 2)
AXES = ("yhi", "core", "z", "x", "ylo")
RING = ("ylo", "yhi")
CHUNKS = ((0, 1), (2,))
ROWS = 4 * LOC
KEYS = 8 * LOC
WIN = 4 * TD
EXP_SCALE = math.log2(math.e) / math.sqrt(HD)


def route(move):
    pairs = []
    for i, at in enumerate(np.ndindex(*SIZES)):
        to = move(*at)
        if to is not None:
            pairs.append((i, int(np.ravel_multi_index(to, SIZES))))
    return pairs


def to_column(distance):
    def move(u, c, z, x, p):
        n = z * 4 + x + distance
        return (u, c, n // 4, n % 4, p) if 0 <= n < COLS else None

    return route(move)


SWAP_CORE = route(lambda u, c, z, x, p: (u, 1 - c, z, x, p))
SWAP_SLAB = route(lambda u, c, z, x, p: (u, c, z, x, 1 - p))
FORWARD = to_column(1)
BACKWARD = to_column(-1)


def pack_kernel(q_ref, k_ref, v_ref, qg_ref, kg_ref, *out_refs):
    for which, (ref, gain) in enumerate(((q_ref, qg_ref), (k_ref, kg_ref), (v_ref, None))):
        for head in range(24):
            part = ref[0, :, head * HD : (head + 1) * HD]
            if gain is not None:
                wide = part.astype(jnp.float32)
                mean = jnp.mean(wide * wide, axis=-1, keepdims=True)
                part = (wide * lax.rsqrt(mean + 1e-06) * gain[...]).astype(jnp.bfloat16)
            for out_ref, heads in zip(out_refs, CHUNKS):
                if head % 3 in heads:
                    at = (head % 3 - heads[0]) * HD
                    out_ref[head // 3, which, 0, :, at : at + HD] = part


def pack(query, key, value, query_gain, key_gain):
    block = pl.BlockSpec((1, LOC, 24 * HD), lambda t: (t, 0, 0))
    gain = pl.BlockSpec((1, HD), lambda t: (0, 0))
    widths = [len(heads) * HD for heads in CHUNKS]
    return pl.pallas_call(
        pack_kernel,
        grid=(TD,),
        in_specs=[block] * 3 + [gain] * 2,
        out_specs=[pl.BlockSpec((8, 3, 1, LOC, w), lambda t: (0, 0, t, 0, 0)) for w in widths],
        out_shape=[jax.ShapeDtypeStruct((8, 3, TD, LOC, w), jnp.bfloat16) for w in widths],
        name="pack",
    )(query, key, value, query_gain.reshape(1, HD), key_gain.reshape(1, HD))


def attend_kernel(
    nh, ids_ref, cnt_ref, own, mate, prev_own, prev_mate, next_own, next_mate, out_ref,
    qbuf, kbuf, vbuf, sbuf, mbuf, lbuf, abuf, sems,
):
    copies = []

    def fetch(src, dst):
        copy = pltpu.make_async_copy(src, dst, sems.at[len(copies)])
        copy.start()
        copies.append(copy)

    for p in range(2):
        for u in range(4):
            rows = slice(u * LOC, (u + 1) * LOC)
            fetch(own.at[p * 4 + u, 0], qbuf.at[p * TD : (p + 1) * TD, rows])
    for half in range(2):
        for u in range(4):
            rows = slice((half * 4 + u) * LOC, (half * 4 + u + 1) * LOC)
            column = (own, mate)[half]
            for kv, buf in enumerate((kbuf, vbuf)):
                for p in range(2):
                    fetch(column.at[p * 4 + u, 1 + kv], buf.at[TD + p * TD : 2 * TD + p * TD, rows])
                fetch((prev_own, prev_mate)[half].at[u, kv], buf.at[0:TD, rows])
                fetch((next_own, next_mate)[half].at[u, kv], buf.at[3 * TD : 4 * TD, rows])
    for copy in copies:
        copy.wait()

    def lanes(h):
        return slice(h * HD, (h + 1) * HD)

    @pl.loop(0, 2 * TD)
    def _(tile):
        count = cnt_ref[tile]
        mbuf[...] = jnp.full_like(mbuf, -1e30)

        @pl.loop(0, count)
        def _(j):
            listed = ids_ref[tile, j]
            for h in range(nh):
                scores = lax.dot_general(
                    qbuf[tile, :, lanes(h)], kbuf[listed, :, lanes(h)],
                    (((1,), (1,)), ((), ())), preferred_element_type=jnp.float32,
                )
                sbuf[h, j] = scores
                top = jnp.maximum(jnp.maximum(scores[:, :128], scores[:, 128:256]), scores[:, 256:])
                mbuf[h] = jnp.maximum(mbuf[h], top)

        for h in range(nh):
            top = jnp.max(mbuf[h], axis=-1, keepdims=True)
            mbuf[h] = jnp.broadcast_to(top, (ROWS, 128))
        lbuf[...] = jnp.zeros_like(lbuf)
        abuf[...] = jnp.zeros_like(abuf)

        @pl.loop(0, count)
        def _(j):
            listed = ids_ref[tile, j]
            for h in range(nh):
                top = mbuf[h]
                parts = [
                    jnp.exp2((sbuf[h, j, :, g * 128 : (g + 1) * 128] - top) * EXP_SCALE)
                    for g in range(3)
                ]
                lbuf[h] += parts[0] + parts[1] + parts[2]
                rounded = jnp.concatenate([part.astype(jnp.bfloat16) for part in parts], axis=-1)
                abuf[h] += jnp.dot(
                    rounded, vbuf[listed, :, lanes(h)], preferred_element_type=jnp.float32
                )

        for h in range(nh):
            total = jnp.sum(lbuf[h], axis=-1, keepdims=True)
            result = (abuf[h] / total).astype(jnp.bfloat16)
            for u in range(4):
                slab = tile // TD
                out_ref[slab * 4 + u, tile % TD, :, lanes(h)] = result[u * LOC : (u + 1) * LOC]


def attend(ids, counts, *arrays):
    width = arrays[0].shape[-1]
    nh = width // HD
    smem = pl.BlockSpec(memory_space=pltpu.SMEM)
    return pl.pallas_call(
        functools.partial(attend_kernel, nh),
        in_specs=[smem] * 2 + [pl.BlockSpec(memory_space=pl.ANY)] * 6,
        out_specs=pl.BlockSpec(memory_space=pltpu.VMEM),
        out_shape=jax.ShapeDtypeStruct((8, TD, LOC, width), jnp.bfloat16),
        scratch_shapes=[
            pltpu.VMEM((2 * TD, ROWS, width), jnp.bfloat16),
            pltpu.VMEM((WIN, KEYS, width), jnp.bfloat16),
            pltpu.VMEM((WIN, KEYS, width), jnp.bfloat16),
            pltpu.VMEM((nh, NB, ROWS, KEYS), jnp.float32),
            pltpu.VMEM((nh, ROWS, 128), jnp.float32),
            pltpu.VMEM((nh, ROWS, 128), jnp.float32),
            pltpu.VMEM((nh, ROWS, HD), jnp.float32),
            pltpu.SemaphoreType.DMA((72,)),
        ],
        compiler_params=pltpu.CompilerParams(vmem_limit_bytes=40 << 20),
        name=f"attend{nh}",
    )(ids, counts, *arrays)


def unpack_kernel(*refs):
    out_ref = refs[-1]
    for ref, heads in zip(refs, CHUNKS):
        width = len(heads) * HD
        for chip in range(8):
            at = chip * 3 * HD + heads[0] * HD
            out_ref[0, :, at : at + width] = ref[chip, 0]


def unpack(*blocks):
    return pl.pallas_call(
        unpack_kernel,
        grid=(TD,),
        in_specs=[
            pl.BlockSpec((8, 1, LOC, b.shape[-1]), lambda t: (0, t, 0, 0)) for b in blocks
        ],
        out_specs=pl.BlockSpec((1, LOC, 24 * HD), lambda t: (t, 0, 0)),
        out_shape=jax.ShapeDtypeStruct((TD, LOC, 24 * HD), jnp.bfloat16),
        name="unpack",
    )(*blocks)


def body(query_proj, key_proj, value_proj, query_gain, key_gain, neighbours, tile_counts):
    slab = lax.axis_index("ylo")
    column = lax.axis_index("z") * SIZES[3] + lax.axis_index("x")
    table = jnp.concatenate([neighbours, tile_counts[:, None]], axis=1)
    other = lax.ppermute(table, AXES, SWAP_SLAB)
    table = jnp.where(slab == 0, jnp.stack([table, other]), jnp.stack([other, table]))
    table = table.reshape(2 * TD, NB + 1)
    ids = table[:, :NB] - (2 * column - 1) * TD
    counts = table[:, NB]

    packed = pack(query_proj, key_proj, value_proj, query_gain, key_gain)
    returned = []
    for block in packed:
        own = lax.all_to_all(block, RING, 0, 0, tiled=True)
        prev_own = lax.ppermute(own[4:, 1:], AXES, FORWARD)
        next_own = lax.ppermute(own[:4, 1:], AXES, BACKWARD)
        mate = lax.ppermute(own, AXES, SWAP_CORE)
        prev_mate = lax.ppermute(prev_own, AXES, SWAP_CORE)
        next_mate = lax.ppermute(next_own, AXES, SWAP_CORE)
        done = attend(ids, counts, own, mate, prev_own, prev_mate, next_own, next_mate)
        returned.append(lax.all_to_all(done, RING, 0, 0, tiled=True))
    return unpack(*returned)


def solution(mesh):
    split = Mesh(mesh.devices.reshape(SIZES), AXES)
    blk, uly = ("z", "x", "ylo"), ("yhi", "core")
    rows = P(blk, uly, None)
    in_specs = (rows, rows, rows, P(), P(), P(blk, None), P(blk))
    return jax.shard_map(body, mesh=split, in_specs=in_specs, out_specs=rows, check_vma=False)
```

```python
import functools
import math

import jax
import jax.numpy as jnp
import numpy as np
from jax import lax
from jax.experimental import pallas as pl
from jax.experimental.pallas import tpu as pltpu
from jax.sharding import Mesh
from jax.sharding import PartitionSpec as P


HD = 128
NB = 9
TD = 3
LOC = 48
COLS = 8 * 4
SIZES = (4, 2, 8, 4, 2)
AXES = ("yhi", "core", "z", "x", "ylo")
RING = ("ylo", "yhi")
CHUNKS = ((0,), (1, 2))
ROWS = 4 * LOC
KEYS = 8 * LOC
GROUP = {1: 9, 2: 3}
STEPS = {"first": 2 * TD, "last": TD, "all": 3 * TD}
EXP_SCALE = math.log2(math.e) / math.sqrt(HD)


def route(move):
    pairs = []
    for i, at in enumerate(np.ndindex(*SIZES)):
        to = move(*at)
        if to is not None:
            pairs.append((i, int(np.ravel_multi_index(to, SIZES))))
    return pairs


def to_column(distance):
    def move(u, c, z, x, p):
        n = z * 4 + x + distance
        return (u, c, n // 4, n % 4, p) if 0 <= n < COLS else None

    return route(move)


SWAP_CORE = route(lambda u, c, z, x, p: (u, 1 - c, z, x, p))
SWAP_SLAB = route(lambda u, c, z, x, p: (u, c, z, x, 1 - p))
FORWARD = to_column(1)
BACKWARD = to_column(-1)


def pack_kernel(heads, q_ref, k_ref, v_ref, qg_ref, kg_ref, out_ref):
    for which, (ref, gain) in enumerate(((q_ref, qg_ref), (k_ref, kg_ref), (v_ref, None))):
        for chip in range(8):
            for slot, head in enumerate(heads):
                at = (chip * 3 + head) * HD
                part = ref[0, :, at : at + HD]
                if gain is not None:
                    wide = part.astype(jnp.float32)
                    mean = jnp.mean(wide * wide, axis=-1, keepdims=True)
                    part = (wide * lax.rsqrt(mean + 1e-06) * gain[...]).astype(jnp.bfloat16)
                out_ref[chip, which, 0, :, slot * HD : (slot + 1) * HD] = part


def pack(heads, query, key, value, query_gain, key_gain):
    width = len(heads) * HD
    block = pl.BlockSpec((1, LOC, 24 * HD), lambda t: (t, 0, 0))
    gain = pl.BlockSpec((1, HD), lambda t: (0, 0))
    return pl.pallas_call(
        functools.partial(pack_kernel, heads),
        grid=(TD,),
        in_specs=[block] * 3 + [gain] * 2,
        out_specs=pl.BlockSpec((8, 3, 1, LOC, width), lambda t: (0, 0, t, 0, 0)),
        out_shape=jax.ShapeDtypeStruct((8, 3, TD, LOC, width), jnp.bfloat16),
    )(query, key, value, query_gain.reshape(1, HD), key_gain.reshape(1, HD))


def attend_kernel(part, nh, live_ref, *refs):
    copies = []
    refs = list(refs)
    sems = refs.pop()
    lbuf, abuf, mbuf, sbuf, vbuf, kbuf, qbuf = (refs.pop() for _ in range(7))
    own = refs.pop(0)
    carry = None
    if part == "first":
        mate = refs.pop(0)
    elif part == "last":
        prev_own, prev_mate, next_own, next_mate = (refs.pop(0) for _ in range(4))
        carry = [refs.pop(0) for _ in range(3)]
    else:
        mate, prev_own, prev_mate, next_own, next_mate = (refs.pop(0) for _ in range(5))
    outs = refs
    tiles = STEPS[part]
    group_size = min(tiles, GROUP[nh])

    def fetch(src, dst):
        copy = pltpu.make_async_copy(src, dst, sems.at[len(copies)])
        copy.start()
        copies.append(copy)

    for p in range(2):
        for u in range(4):
            rows = slice(u * LOC, (u + 1) * LOC)
            fetch(own.at[p * 4 + u, 0], qbuf.at[p * TD : (p + 1) * TD, rows])
    for half in range(2):
        for u in range(4):
            rows = slice((half * 4 + u) * LOC, (half * 4 + u + 1) * LOC)
            for kv, buf in enumerate((kbuf, vbuf)):
                parts = []
                if part != "first":
                    parts.append((prev_own, prev_mate)[half].at[u, kv])
                if part != "last":
                    column = (own, mate)[half]
                    parts += [column.at[u, 1 + kv], column.at[4 + u, 1 + kv]]
                if part != "first":
                    parts.append((next_own, next_mate)[half].at[u, kv])
                for slab, src in enumerate(parts):
                    fetch(src, buf.at[slab * TD : (slab + 1) * TD, rows])
    for copy in copies:
        copy.wait()

    def lanes(h):
        return slice(h * HD, (h + 1) * HD)

    def key_tile(tile, j):
        return j if part == "first" else tile // TD * TD + j

    def is_live(tile, j):
        slab = tile // TD
        at = {"first": j + TD * (1 - slab), "last": j + 2 * TD * slab, "all": j}[part]
        return live_ref[tile, at] > 0

    def step(group, tile, ahead):
        for i in range(group_size):
            j = group * group_size + i
            if tile is not None:
                listed = key_tile(tile, j)
                live = is_live(tile, j)
                slot = tile % 2
                for h in range(nh):
                    top = jnp.where(live, mbuf[slot, h], 1e30)
                    parts = [
                        jnp.exp2((sbuf[slot, h, j, :, lanes(g)] - top) * EXP_SCALE)
                        for g in range(KEYS // 128)
                    ]
                    lbuf[h] += sum(parts[1:], parts[0])
                    rounded = jnp.concatenate([p.astype(jnp.bfloat16) for p in parts], axis=-1)
                    abuf[h] += jnp.dot(
                        rounded, vbuf[listed, :, lanes(h)], preferred_element_type=jnp.float32
                    )
            if ahead is not None:
                listed = key_tile(ahead, j)
                live = is_live(ahead, j)
                slot = ahead % 2
                for h in range(nh):
                    scores = lax.dot_general(
                        qbuf[ahead, :, lanes(h)], kbuf[listed, :, lanes(h)],
                        (((1,), (1,)), ((), ())), preferred_element_type=jnp.float32,
                    )
                    sbuf[slot, h, j] = scores
                    top = functools.reduce(
                        jnp.maximum, [scores[:, lanes(g)] for g in range(KEYS // 128)]
                    )
                    mbuf[slot, h] = jnp.maximum(mbuf[slot, h], jnp.where(live, top, -1e30))

    def sweep(tile, ahead):
        if tile is not None:
            for h in range(nh):
                if carry is None:
                    lbuf[h] = jnp.zeros(lbuf.shape[1:], jnp.float32)
                    abuf[h] = jnp.zeros(abuf.shape[1:], jnp.float32)
                else:
                    top, total, sums = (ref[tile, h] for ref in carry)
                    scale = jnp.exp2((top - mbuf[tile % 2, h]) * EXP_SCALE)
                    lbuf[h] = total * scale
                    abuf[h] = sums * scale
        if ahead is not None:
            if carry is None:
                mbuf[ahead % 2] = jnp.full(mbuf.shape[1:], -1e30, jnp.float32)
            else:
                mbuf[ahead % 2] = carry[0][ahead]

        @pl.loop(0, tiles // group_size)
        def _(group):
            step(group, tile, ahead)

        for h in range(nh):
            if ahead is not None:
                top = jnp.max(mbuf[ahead % 2, h], axis=-1, keepdims=True)
                mbuf[ahead % 2, h] = jnp.broadcast_to(top, (ROWS, 128))
            if tile is not None and part == "first":
                outs[0][tile, h] = mbuf[tile % 2, h]
                outs[1][tile, h] = lbuf[h]
                outs[2][tile, h] = abuf[h]
            elif tile is not None:
                total = jnp.sum(lbuf[h], axis=-1, keepdims=True)
                result = (abuf[h] / total).astype(jnp.bfloat16)
                for u in range(4):
                    at = tile // TD * 4 + u
                    outs[0][at, tile % TD, :, lanes(h)] = result[u * LOC : (u + 1) * LOC]

    sweep(None, 0)

    @pl.loop(0, 2 * TD - 1)
    def _(tile):
        sweep(tile, tile + 1)

    sweep(2 * TD - 1, None)


def attend(part, live, arrays, carry=()):
    width = arrays[0].shape[-1]
    nh = width // HD
    whole = pl.BlockSpec(memory_space=pltpu.VMEM)
    if part == "first":
        shapes = [jax.ShapeDtypeStruct((2 * TD, nh, ROWS, 128), jnp.float32)] * 3
    else:
        shapes = [jax.ShapeDtypeStruct((8, TD, LOC, width), jnp.bfloat16)]
    held = {"first": 2, "last": 2, "all": 4}[part] * TD
    return pl.pallas_call(
        functools.partial(attend_kernel, part, nh),
        in_specs=[pl.BlockSpec(memory_space=pltpu.SMEM)]
        + [pl.BlockSpec(memory_space=pl.ANY)] * len(arrays)
        + [whole] * len(carry),
        out_specs=[whole] * len(shapes),
        out_shape=shapes,
        scratch_shapes=[
            pltpu.VMEM((2 * TD, ROWS, width), jnp.bfloat16),
            pltpu.VMEM((held, KEYS, width), jnp.bfloat16),
            pltpu.VMEM((held, KEYS, width), jnp.bfloat16),
            pltpu.VMEM((2, nh, STEPS[part], ROWS, KEYS), jnp.float32),
            pltpu.VMEM((2, nh, ROWS, 128), jnp.float32),
            pltpu.VMEM((nh, ROWS, HD), jnp.float32),
            pltpu.VMEM((nh, ROWS, 128), jnp.float32),
            pltpu.SemaphoreType.DMA((72,)),
        ],
        compiler_params=pltpu.CompilerParams(vmem_limit_bytes=24 << 20),
    )(live, *arrays, *carry)


def unpack_kernel(*refs):
    out_ref = refs[-1]
    for ref, heads in zip(refs, CHUNKS):
        width = len(heads) * HD
        for chip in range(8):
            at = (chip * 3 + heads[0]) * HD
            out_ref[0, :, at : at + width] = ref[chip, 0]


def unpack(*blocks):
    return pl.pallas_call(
        unpack_kernel,
        grid=(TD,),
        in_specs=[
            pl.BlockSpec((8, 1, LOC, b.shape[-1]), lambda t: (0, t, 0, 0)) for b in blocks
        ],
        out_specs=pl.BlockSpec((1, LOC, 24 * HD), lambda t: (t, 0, 0)),
        out_shape=jax.ShapeDtypeStruct((TD, LOC, 24 * HD), jnp.bfloat16),
        name="unpack",
    )(*blocks)


def compute(query_proj, key_proj, value_proj, query_gain, key_gain, neighbours, tile_counts):
    slab = lax.axis_index("ylo")
    column = lax.axis_index("z") * SIZES[3] + lax.axis_index("x")
    table = jnp.concatenate([neighbours, tile_counts[:, None]], axis=1)
    other = lax.ppermute(table, AXES, SWAP_SLAB)
    table = jnp.where(slab == 0, jnp.stack([table, other]), jnp.stack([other, table]))
    table = table.reshape(2 * TD, NB + 1)
    first_tile = (2 * column - 1) * TD + TD * (jnp.arange(2 * TD, dtype=jnp.int32) // TD)
    local = table[:, :NB] - first_tile[:, None]
    place = jnp.arange(NB, dtype=jnp.int32)
    counted = place[None, :] < table[:, NB:]
    match = (local[:, None, :] == place[None, :, None]) & counted[:, None, :]
    live = jnp.any(match, axis=2).astype(jnp.int32)

    returned = []
    for i, heads in enumerate(CHUNKS):
        block = pack(heads, query_proj, key_proj, value_proj, query_gain, key_gain)
        own = lax.all_to_all(block, RING, 0, 0, tiled=True)
        prev_own = lax.ppermute(own[4:, 1:], AXES, FORWARD)
        next_own = lax.ppermute(own[:4, 1:], AXES, BACKWARD)
        mate = lax.ppermute(own, AXES, SWAP_CORE)
        prev_mate = lax.ppermute(prev_own, AXES, SWAP_CORE)
        next_mate = lax.ppermute(next_own, AXES, SWAP_CORE)
        halo = [prev_own, prev_mate, next_own, next_mate]
        if i == len(CHUNKS) - 1:
            carry = attend("first", live, [own, mate])
            (done,) = attend("last", live, [own, *halo], carry)
        else:
            (done,) = attend("all", live, [own, mate, *halo])
        returned.append(lax.all_to_all(done, RING, 0, 0, tiled=True))
    return unpack(*returned)


def solution(mesh):
    split = Mesh(mesh.devices.reshape(SIZES), AXES)
    blk, uly = ("z", "x", "ylo"), ("yhi", "core")
    rows = P(blk, uly, None)
    in_specs = (rows, rows, rows, P(), P(), P(blk, None), P(blk))
    return jax.shard_map(compute, mesh=split, in_specs=in_specs, out_specs=rows, check_vma=False)
```

```python
import functools
import math

import jax
import jax.numpy as jnp
import numpy as np
from jax import lax
from jax.experimental import pallas as pl
from jax.experimental.pallas import tpu as pltpu
from jax.sharding import Mesh
from jax.sharding import PartitionSpec as P


HD = 128
NB = 9
TD = 3
LOC = 48
COLS = 8 * 4
SIZES = (4, 2, 8, 4, 2)
AXES = ("yhi", "core", "z", "x", "ylo")
RING = ("ylo", "yhi")
CHUNKS = ((0,), (1, 2))
ROWS = 4 * LOC
KEYS = 8 * LOC
SLABS = {"first": 2, "last": 1, "all": 3}
EXP_SCALE = math.log2(math.e) / math.sqrt(HD)


def route(move):
    pairs = []
    for i, at in enumerate(np.ndindex(*SIZES)):
        to = move(*at)
        if to is not None:
            pairs.append((i, int(np.ravel_multi_index(to, SIZES))))
    return pairs


def to_column(distance):
    def move(u, c, z, x, p):
        n = z * 4 + x + distance
        return (u, c, n // 4, n % 4, p) if 0 <= n < COLS else None

    return route(move)


SWAP_CORE = route(lambda u, c, z, x, p: (u, 1 - c, z, x, p))
SWAP_SLAB = route(lambda u, c, z, x, p: (u, c, z, x, 1 - p))
FORWARD = to_column(1)
BACKWARD = to_column(-1)


def pack_kernel(heads, q_ref, k_ref, v_ref, qg_ref, kg_ref, out_ref):
    for which, (ref, gain) in enumerate(((q_ref, qg_ref), (k_ref, kg_ref), (v_ref, None))):
        for chip in range(8):
            for slot, head in enumerate(heads):
                at = (chip * 3 + head) * HD
                part = ref[:, :, at : at + HD]
                if gain is not None:
                    wide = part.astype(jnp.float32)
                    mean = jnp.mean(wide * wide, axis=-1, keepdims=True)
                    part = (wide * lax.rsqrt(mean + 1e-06) * gain[...]).astype(jnp.bfloat16)
                out_ref[chip, which, :, :, slot * HD : (slot + 1) * HD] = part


def pack(heads, query, key, value, query_gain, key_gain):
    width = len(heads) * HD
    whole = pl.BlockSpec(memory_space=pltpu.VMEM)
    return pl.pallas_call(
        functools.partial(pack_kernel, heads),
        in_specs=[whole] * 5,
        out_specs=whole,
        out_shape=jax.ShapeDtypeStruct((8, 3, TD, LOC, width), jnp.bfloat16),
    )(query, key, value, query_gain.reshape(1, HD), key_gain.reshape(1, HD))


def attend_kernel(part, nh, live_ref, *refs):
    copies = []
    refs = list(refs)
    sems = refs.pop()
    lbuf, abuf, mbuf, sbuf, vbuf, kbuf, qbuf = (refs.pop() for _ in range(7))
    own = refs.pop(0)
    carry = None
    if part == "first":
        mate = refs.pop(0)
    elif part == "last":
        prev_own, prev_mate, next_own, next_mate = (refs.pop(0) for _ in range(4))
        carry = [refs.pop(0) for _ in range(3)]
    else:
        mate, prev_own, prev_mate, next_own, next_mate = (refs.pop(0) for _ in range(5))
    early = refs.pop(0) if len(refs) == 2 else None
    outs = refs
    base = 0 if early is None else early.shape[-1]
    groups = SLABS[part]

    def fetch(src, dst):
        copy = pltpu.make_async_copy(src, dst, sems.at[len(copies)])
        copy.start()
        copies.append(copy)

    for p in range(2):
        for u in range(4):
            rows = slice(u * LOC, (u + 1) * LOC)
            fetch(own.at[p * 4 + u, 0], qbuf.at[p * TD : (p + 1) * TD, rows])
    for half in range(2):
        for u in range(4):
            rows = slice((half * 4 + u) * LOC, (half * 4 + u + 1) * LOC)
            for kv, buf in enumerate((kbuf, vbuf)):
                parts = []
                if part != "first":
                    parts.append((prev_own, prev_mate)[half].at[u, kv])
                if part != "last":
                    column = (own, mate)[half]
                    parts += [column.at[u, 1 + kv], column.at[4 + u, 1 + kv]]
                if part != "first":
                    parts.append((next_own, next_mate)[half].at[u, kv])
                for slab, src in enumerate(parts):
                    fetch(src, buf.at[slab * TD : (slab + 1) * TD, rows])
    for copy in copies:
        copy.wait()

    def lanes(h):
        return slice(h * HD, (h + 1) * HD)

    def keys(buf, tile, group, h):
        slab = group if part == "first" else tile // TD + group
        rows = buf[pl.ds(slab * TD, TD), :, lanes(h)]
        return rows.reshape(TD * KEYS, HD)

    def is_live(tile, group, i):
        slab = tile // TD
        at = {"first": group + 1 - slab, "last": 2 * slab, "all": group}[part]
        return live_ref[tile, at * TD + i] > 0

    def score(tile, group, heads):
        for h in heads:
            scores = lax.dot_general(
                qbuf[tile, :, lanes(h)], keys(kbuf, tile, group, h),
                (((1,), (1,)), ((), ())), preferred_element_type=jnp.float32,
            ) * EXP_SCALE
            sbuf[h, group] = scores
            best = mbuf[h]
            for i in range(TD):
                top = functools.reduce(
                    jnp.maximum, [scores[:, lanes(i * 3 + g)] for g in range(3)]
                )
                best = jnp.maximum(best, jnp.where(is_live(tile, group, i), top, -1e30))
            mbuf[h] = best

    def weigh(tile, group, heads):
        for h in heads:
            best = mbuf[h]
            values = keys(vbuf, tile, group, h)
            for i in range(TD):
                top = jnp.where(is_live(tile, group, i), best, 1e30)
                parts = [jnp.exp2(sbuf[h, group, :, lanes(i * 3 + g)] - top) for g in range(3)]
                lbuf[h] += parts[0] + parts[1] + parts[2]
                abuf[h] += jnp.dot(
                    jnp.concatenate([p.astype(jnp.bfloat16) for p in parts], axis=-1),
                    values[i * KEYS : (i + 1) * KEYS], preferred_element_type=jnp.float32,
                )

    @pl.loop(0, 2 * TD)
    def _(tile):
        for h in range(nh):
            if carry is None:
                mbuf[h] = jnp.full(mbuf.shape[1:], -1e30, jnp.float32)
            else:
                mbuf[h] = carry[0][tile, h]

        for group in range(groups):
            score(tile, group, range(nh))

        for h in range(nh):
            top = jnp.max(mbuf[h], axis=-1, keepdims=True)
            mbuf[h] = jnp.broadcast_to(top, (ROWS, 128))
            if carry is None:
                lbuf[h] = jnp.zeros(lbuf.shape[1:], jnp.float32)
                abuf[h] = jnp.zeros(abuf.shape[1:], jnp.float32)
            else:
                scale = jnp.exp2(carry[0][tile, h] - mbuf[h])
                lbuf[h] = carry[1][tile, h] * scale
                abuf[h] = carry[2][tile, h] * scale

        for group in range(groups):
            weigh(tile, group, range(nh))

        for h in range(nh):
            if part == "first":
                outs[0][tile, h] = mbuf[h]
                outs[1][tile, h] = lbuf[h]
                outs[2][tile, h] = abuf[h]
            else:
                total = jnp.sum(lbuf[h], axis=-1, keepdims=True)
                result = (abuf[h] / total).astype(jnp.bfloat16)
                for u in range(4):
                    at = tile // TD * 4 + u
                    where = slice(base + h * HD, base + (h + 1) * HD)
                    outs[0][at, tile % TD, :, where] = result[u * LOC : (u + 1) * LOC]

    if early is not None:
        outs[0][:, :, :, :base] = early[...]


def attend(part, live, arrays, carry=(), early=()):
    width = arrays[0].shape[-1]
    nh = width // HD
    whole = pl.BlockSpec(memory_space=pltpu.VMEM)
    if part == "first":
        shapes = [jax.ShapeDtypeStruct((2 * TD, nh, ROWS, 128), jnp.float32)] * 3
    else:
        both = width + sum(block.shape[-1] for block in early)
        shapes = [jax.ShapeDtypeStruct((8, TD, LOC, both), jnp.bfloat16)]
    held = {"first": 2, "last": 2, "all": 4}[part] * TD
    return pl.pallas_call(
        functools.partial(attend_kernel, part, nh),
        in_specs=[pl.BlockSpec(memory_space=pltpu.SMEM)]
        + [pl.BlockSpec(memory_space=pl.ANY)] * len(arrays)
        + [whole] * (len(carry) + len(early)),
        out_specs=[whole] * len(shapes),
        out_shape=shapes,
        scratch_shapes=[
            pltpu.VMEM((2 * TD, ROWS, width), jnp.bfloat16),
            pltpu.VMEM((held, KEYS, width), jnp.bfloat16),
            pltpu.VMEM((held, KEYS, width), jnp.bfloat16),
            pltpu.VMEM((nh, SLABS[part], ROWS, TD * KEYS), jnp.float32),
            pltpu.VMEM((nh, ROWS, 128), jnp.float32),
            pltpu.VMEM((nh, ROWS, HD), jnp.float32),
            pltpu.VMEM((nh, ROWS, 128), jnp.float32),
            pltpu.SemaphoreType.DMA((72,)),
        ],
        compiler_params=pltpu.CompilerParams(vmem_limit_bytes=24 << 20),
    )(live, *arrays, *carry, *early)


def unpack_kernel(ref, out_ref):
    width = ref.shape[-1]
    for chip in range(8):
        out_ref[:, :, chip * width : (chip + 1) * width] = ref[chip]


def unpack(block):
    whole = pl.BlockSpec(memory_space=pltpu.VMEM)
    return pl.pallas_call(
        unpack_kernel,
        in_specs=[whole],
        out_specs=whole,
        out_shape=jax.ShapeDtypeStruct((TD, LOC, 24 * HD), jnp.bfloat16),
        name="unpack",
    )(block)


def compute(query_proj, key_proj, value_proj, query_gain, key_gain, neighbours, tile_counts):
    slab = lax.axis_index("ylo")
    column = lax.axis_index("z") * SIZES[3] + lax.axis_index("x")
    table = jnp.concatenate([neighbours, tile_counts[:, None]], axis=1)
    other = lax.ppermute(table, AXES, SWAP_SLAB)
    table = jnp.where(slab == 0, jnp.stack([table, other]), jnp.stack([other, table]))
    table = table.reshape(2 * TD, NB + 1)
    first_tile = (2 * column - 1) * TD + TD * (jnp.arange(2 * TD, dtype=jnp.int32) // TD)
    local = table[:, :NB] - first_tile[:, None]
    place = jnp.arange(NB, dtype=jnp.int32)
    counted = place[None, :] < table[:, NB:]
    match = (local[:, None, :] == place[None, :, None]) & counted[:, None, :]
    live = jnp.any(match, axis=2).astype(jnp.int32)

    early = ()
    for i, heads in enumerate(CHUNKS):
        block = pack(heads, query_proj, key_proj, value_proj, query_gain, key_gain)
        own = lax.all_to_all(block, RING, 0, 0, tiled=True)
        prev_own = lax.ppermute(own[4:, 1:], AXES, FORWARD)
        next_own = lax.ppermute(own[:4, 1:], AXES, BACKWARD)
        mate = lax.ppermute(own, AXES, SWAP_CORE)
        prev_mate = lax.ppermute(prev_own, AXES, SWAP_CORE)
        next_mate = lax.ppermute(next_own, AXES, SWAP_CORE)
        halo = [prev_own, prev_mate, next_own, next_mate]
        if i == len(CHUNKS) - 1:
            carry = attend("first", live, [own, mate])
            (done,) = attend("last", live, [own, *halo], carry, early)
        else:
            early = attend("all", live, [own, mate, *halo])
    done = lax.all_to_all(done, RING, 0, 0, tiled=True)
    return unpack(done)


def solution(mesh):
    split = Mesh(mesh.devices.reshape(SIZES), AXES)
    blk, uly = ("z", "x", "ylo"), ("yhi", "core")
    rows = P(blk, uly, None)
    in_specs = (rows, rows, rows, P(), P(), P(blk, None), P(blk))
    return jax.shard_map(compute, mesh=split, in_specs=in_specs, out_specs=rows, check_vma=False)
```

```python
import functools
import math

import jax
import jax.numpy as jnp
import numpy as np
from jax import lax
from jax.experimental import pallas as pl
from jax.experimental.pallas import tpu as pltpu
from jax.sharding import Mesh
from jax.sharding import PartitionSpec as P


HD = 128
NB = 9
TD = 3
LOC = 48
COLS = 8 * 4
SIZES = (4, 2, 8, 4, 2)
AXES = ("yhi", "core", "z", "x", "ylo")
RING = ("ylo", "yhi")
HEADS = 3
ROWS = 4 * LOC
KEYS = 8 * LOC
SLABS = {"first": 2, "last": 1}
EXP_SCALE = math.log2(math.e) / math.sqrt(HD)


def route(move):
    pairs = []
    for i, at in enumerate(np.ndindex(*SIZES)):
        to = move(*at)
        if to is not None:
            pairs.append((i, int(np.ravel_multi_index(to, SIZES))))
    return pairs


def to_column(distance):
    def move(u, c, z, x, p):
        n = z * 4 + x + distance
        return (u, c, n // 4, n % 4, p) if 0 <= n < COLS else None

    return route(move)


SWAP_CORE = route(lambda u, c, z, x, p: (u, 1 - c, z, x, p))
SWAP_SLAB = route(lambda u, c, z, x, p: (u, c, z, x, 1 - p))
FORWARD = to_column(1)
BACKWARD = to_column(-1)


def pack_kernel(normed, *refs):
    out_ref = refs[-1]
    refs = list(refs[:-1])
    for which, has_gain in enumerate(normed):
        ref = refs.pop(0)
        gain = refs.pop(0) if has_gain else None
        for chip in range(8):
            for head in range(HEADS):
                at = (chip * HEADS + head) * HD
                part = ref[:, :, at : at + HD]
                if has_gain:
                    wide = part.astype(jnp.float32)
                    mean = jnp.mean(wide * wide, axis=-1, keepdims=True)
                    part = (wide * lax.rsqrt(mean + 1e-06) * gain[...]).astype(jnp.bfloat16)
                out_ref[chip, which, :, :, head * HD : (head + 1) * HD] = part


def pack(*pairs):
    whole = pl.BlockSpec(memory_space=pltpu.VMEM)
    operands = []
    for array, gain in pairs:
        operands += [array] if gain is None else [array, gain.reshape(1, HD)]
    shape = (8, len(pairs), TD, LOC, HEADS * HD)
    return pl.pallas_call(
        functools.partial(pack_kernel, [gain is not None for _, gain in pairs]),
        in_specs=[whole] * len(operands),
        out_specs=whole,
        out_shape=jax.ShapeDtypeStruct(shape, jnp.bfloat16),
    )(*operands)


def attend_kernel(part, nh, live_ref, query, *refs):
    refs = list(refs)
    lbuf, abuf, mbuf, sbuf = (refs.pop() for _ in range(4))
    column = (refs.pop(0), refs.pop(0)) if part == "first" else None
    before = (refs.pop(0), refs.pop(0)) if part == "last" else None
    after = (refs.pop(0), refs.pop(0)) if part == "last" else None
    carry = [refs.pop(0) for _ in range(3)] if part == "last" else None
    outs = refs

    def lanes(h):
        return slice(h * HD, (h + 1) * HD)

    def slabs(p):
        if part == "first":
            return [(column, 0, 1 - p), (column, 4, 2 - p)]
        return [(before, 0, 0)] if p == 0 else [(after, 0, 2)]

    def key_tile(slab, kv, t, h):
        arrays, first, _ = slab
        pieces = [a[first + u, kv, t, :, lanes(h)] for a in arrays for u in range(4)]
        return jnp.concatenate(pieces, axis=0)

    def query_tile(p, t, h):
        return jnp.concatenate([query[p * 4 + u, 0, t, :, lanes(h)] for u in range(4)], axis=0)

    def score(p, t, group, slab, h):
        keys = jnp.concatenate([key_tile(slab, 0, i, h) for i in range(TD)], axis=0)
        scores = lax.dot_general(
            query_tile(p, t, h), keys,
            (((1,), (1,)), ((), ())), preferred_element_type=jnp.float32,
        ) * EXP_SCALE
        sbuf[h, group] = scores
        best = mbuf[h]
        for i in range(TD):
            live = live_ref[p * TD + t, slab[2] * TD + i] > 0
            top = functools.reduce(jnp.maximum, [scores[:, lanes(i * 3 + g)] for g in range(3)])
            best = jnp.maximum(best, jnp.where(live, top, -1e30))
        mbuf[h] = best

    def weigh(p, t, group, slab, h):
        best = mbuf[h]
        for i in range(TD):
            live = live_ref[p * TD + t, slab[2] * TD + i] > 0
            top = jnp.where(live, best, 1e30)
            parts = [jnp.exp2(sbuf[h, group, :, lanes(i * 3 + g)] - top) for g in range(3)]
            lbuf[h] += parts[0] + parts[1] + parts[2]
            abuf[h] += jnp.dot(
                jnp.concatenate([w.astype(jnp.bfloat16) for w in parts], axis=-1),
                key_tile(slab, 1, i, h), preferred_element_type=jnp.float32,
            )

    def attend_tile(p, t):
        tile = p * TD + t
        for h in range(nh):
            if carry is None:
                mbuf[h] = jnp.full(mbuf.shape[1:], -1e30, jnp.float32)
            else:
                mbuf[h] = carry[0][tile, h]
        for group, slab in enumerate(slabs(p)):
            for h in range(nh):
                score(p, t, group, slab, h)
        for h in range(nh):
            top = jnp.max(mbuf[h], axis=-1, keepdims=True)
            mbuf[h] = jnp.broadcast_to(top, (ROWS, 128))
            if carry is None:
                lbuf[h] = jnp.zeros(lbuf.shape[1:], jnp.float32)
                abuf[h] = jnp.zeros(abuf.shape[1:], jnp.float32)
            else:
                scale = jnp.exp2(carry[0][tile, h] - mbuf[h])
                lbuf[h] = carry[1][tile, h] * scale
                abuf[h] = carry[2][tile, h] * scale
        for group, slab in enumerate(slabs(p)):
            for h in range(nh):
                weigh(p, t, group, slab, h)
        for h in range(nh):
            if part == "first":
                outs[0][tile, h] = mbuf[h]
                outs[1][tile, h] = lbuf[h]
                outs[2][tile, h] = abuf[h]
            else:
                total = jnp.sum(lbuf[h], axis=-1, keepdims=True)
                result = (abuf[h] / total).astype(jnp.bfloat16)
                for u in range(4):
                    outs[0][p * 4 + u, t, :, lanes(h)] = result[u * LOC : (u + 1) * LOC]

    for p in range(2):

        @pl.loop(0, TD)
        def _(t):
            attend_tile(p, t)


def attend(part, live, arrays, carry=()):
    width = arrays[0].shape[-1]
    nh = width // HD
    whole = pl.BlockSpec(memory_space=pltpu.VMEM)
    if part == "first":
        shapes = [jax.ShapeDtypeStruct((2 * TD, nh, ROWS, 128), jnp.float32)] * 3
    else:
        shapes = [jax.ShapeDtypeStruct((8, TD, LOC, width), jnp.bfloat16)]
    return pl.pallas_call(
        functools.partial(attend_kernel, part, nh),
        in_specs=[pl.BlockSpec(memory_space=pltpu.SMEM)]
        + [whole] * (len(arrays) + len(carry)),
        out_specs=[whole] * len(shapes),
        out_shape=shapes,
        scratch_shapes=[
            pltpu.VMEM((nh, SLABS[part], ROWS, TD * KEYS), jnp.float32),
            pltpu.VMEM((nh, ROWS, 128), jnp.float32),
            pltpu.VMEM((nh, ROWS, HD), jnp.float32),
            pltpu.VMEM((nh, ROWS, 128), jnp.float32),
        ],
        compiler_params=pltpu.CompilerParams(vmem_limit_bytes=32 << 20),
    )(live, *arrays, *carry)


def unpack_kernel(ref, out_ref):
    width = ref.shape[-1]
    for chip in range(8):
        out_ref[:, :, chip * width : (chip + 1) * width] = ref[chip]


def unpack(block):
    whole = pl.BlockSpec(memory_space=pltpu.VMEM)
    return pl.pallas_call(
        unpack_kernel,
        in_specs=[whole],
        out_specs=whole,
        out_shape=jax.ShapeDtypeStruct((TD, LOC, 24 * HD), jnp.bfloat16),
        name="unpack",
    )(block)


def compute(query_proj, key_proj, value_proj, query_gain, key_gain, neighbours, tile_counts):
    slab = lax.axis_index("ylo")
    column = lax.axis_index("z") * SIZES[3] + lax.axis_index("x")
    table = jnp.concatenate([neighbours, tile_counts[:, None]], axis=1)
    other = lax.ppermute(table, AXES, SWAP_SLAB)
    table = jnp.where(slab == 0, jnp.stack([table, other]), jnp.stack([other, table]))
    table = table.reshape(2 * TD, NB + 1)
    first_tile = (2 * column - 1) * TD + TD * (jnp.arange(2 * TD, dtype=jnp.int32) // TD)
    local = table[:, :NB] - first_tile[:, None]
    place = jnp.arange(NB, dtype=jnp.int32)
    counted = place[None, :] < table[:, NB:]
    match = (local[:, None, :] == place[None, :, None]) & counted[:, None, :]
    live = jnp.any(match, axis=2).astype(jnp.int32)

    block = pack((key_proj, key_gain), (value_proj, None))
    own = lax.all_to_all(block, RING, 0, 0, tiled=True)
    block = pack((query_proj, query_gain))
    query = lax.all_to_all(block, RING, 0, 0, tiled=True)
    prev_own = lax.ppermute(own[4:], AXES, FORWARD)
    next_own = lax.ppermute(own[:4], AXES, BACKWARD)
    mate = lax.ppermute(own, AXES, SWAP_CORE)
    prev_mate = lax.ppermute(prev_own, AXES, SWAP_CORE)
    next_mate = lax.ppermute(next_own, AXES, SWAP_CORE)
    carry = attend("first", live, [query, own, mate])
    halo = [prev_own, prev_mate, next_own, next_mate]
    (done,) = attend("last", live, [query, *halo], carry)
    done = lax.all_to_all(done, RING, 0, 0, tiled=True)
    return unpack(done)


def solution(mesh):
    split = Mesh(mesh.devices.reshape(SIZES), AXES)
    blk, uly = ("z", "x", "ylo"), ("yhi", "core")
    rows = P(blk, uly, None)
    in_specs = (rows, rows, rows, P(), P(), P(blk, None), P(blk))
    return jax.shard_map(compute, mesh=split, in_specs=in_specs, out_specs=rows, check_vma=False)
```

```python
import functools
import math

import jax
import jax.numpy as jnp
import numpy as np
from jax import lax
from jax.experimental import pallas as pl
from jax.experimental.pallas import tpu as pltpu
from jax.sharding import Mesh
from jax.sharding import PartitionSpec as P


HD = 128
NB = 9
TD = 3
LOC = 48
COLS = 8 * 4
SIZES = (4, 2, 8, 4, 2)
AXES = ("yhi", "core", "z", "x", "ylo")
RING = ("ylo", "yhi")
HEADS = 3
AT_ONCE = 4
ROWS = 4 * LOC
KEYS = 8 * LOC
SLABS = {"first": 2, "last": 1}
EXP_SCALE = math.log2(math.e) / math.sqrt(HD)


def route(move):
    pairs = []
    for i, at in enumerate(np.ndindex(*SIZES)):
        to = move(*at)
        if to is not None:
            pairs.append((i, int(np.ravel_multi_index(to, SIZES))))
    return pairs


def to_column(distance):
    def move(u, c, z, x, p):
        n = z * 4 + x + distance
        return (u, c, n // 4, n % 4, p) if 0 <= n < COLS else None

    return route(move)


SWAP_CORE = route(lambda u, c, z, x, p: (u, 1 - c, z, x, p))
SWAP_SLAB = route(lambda u, c, z, x, p: (u, c, z, x, 1 - p))
FORWARD = to_column(1)
BACKWARD = to_column(-1)


def pack_kernel(normed, *refs):
    out_ref = refs[-1]
    refs = list(refs[:-1])
    for which, has_gain in enumerate(normed):
        ref = refs.pop(0)
        gain = refs.pop(0) if has_gain else None
        for chip in range(AT_ONCE):
            for head in range(HEADS):
                at = (chip * HEADS + head) * HD
                part = ref[:, :, at : at + HD]
                if has_gain:
                    wide = part.astype(jnp.float32)
                    mean = jnp.mean(wide * wide, axis=-1, keepdims=True)
                    part = (wide * lax.rsqrt(mean + 1e-06) * gain[...]).astype(jnp.bfloat16)
                out_ref[chip, which, :, :, head * HD : (head + 1) * HD] = part


def pack(*pairs):
    width = AT_ONCE * HEADS * HD
    operands, specs = [], []
    for array, gain in pairs:
        operands += [array] if gain is None else [array, gain.reshape(1, HD)]
        specs.append(pl.BlockSpec((TD, LOC, width), lambda i: (0, 0, i)))
        if gain is not None:
            specs.append(pl.BlockSpec((1, HD), lambda i: (0, 0)))
    shape = (8, len(pairs), TD, LOC, HEADS * HD)
    return pl.pallas_call(
        functools.partial(pack_kernel, [gain is not None for _, gain in pairs]),
        grid=(8 // AT_ONCE,),
        in_specs=specs,
        out_specs=pl.BlockSpec((AT_ONCE,) + shape[1:], lambda i: (i, 0, 0, 0, 0)),
        out_shape=jax.ShapeDtypeStruct(shape, jnp.bfloat16),
    )(*operands)


def attend_kernel(part, nh, live_ref, query, *refs):
    refs = list(refs)
    lbuf, abuf, mbuf, sbuf = (refs.pop() for _ in range(4))
    column = (refs.pop(0), refs.pop(0)) if part == "first" else None
    before = (refs.pop(0), refs.pop(0)) if part == "last" else None
    after = (refs.pop(0), refs.pop(0)) if part == "last" else None
    carry = [refs.pop(0) for _ in range(3)] if part == "last" else None
    outs = refs

    def lanes(h):
        return slice(h * HD, (h + 1) * HD)

    def slabs(p):
        if part == "first":
            return [(column, 0, 1 - p), (column, 4, 2 - p)]
        return [(before, 0, 0)] if p == 0 else [(after, 0, 2)]

    def key_tile(slab, kv, t, h):
        arrays, first, _ = slab
        pieces = [a[first + u, kv, t, :, lanes(h)] for a in arrays for u in range(4)]
        return jnp.concatenate(pieces, axis=0)

    def query_tile(p, t, h):
        return jnp.concatenate([query[p * 4 + u, 0, t, :, lanes(h)] for u in range(4)], axis=0)

    def score(p, t, group, slab, h):
        keys = jnp.concatenate([key_tile(slab, 0, i, h) for i in range(TD)], axis=0)
        scores = lax.dot_general(
            query_tile(p, t, h), keys,
            (((1,), (1,)), ((), ())), preferred_element_type=jnp.float32,
        ) * EXP_SCALE
        sbuf[h, group] = scores
        best = mbuf[h]
        for i in range(TD):
            live = live_ref[p * TD + t, slab[2] * TD + i] > 0
            top = functools.reduce(jnp.maximum, [scores[:, lanes(i * 3 + g)] for g in range(3)])
            best = jnp.maximum(best, jnp.where(live, top, -1e30))
        mbuf[h] = best

    def weigh(p, t, group, slab, h):
        best = mbuf[h]
        for i in range(TD):
            live = live_ref[p * TD + t, slab[2] * TD + i] > 0
            top = jnp.where(live, best, 1e30)
            parts = [jnp.exp2(sbuf[h, group, :, lanes(i * 3 + g)] - top) for g in range(3)]
            lbuf[h] += parts[0] + parts[1] + parts[2]
            abuf[h] += jnp.dot(
                jnp.concatenate([w.astype(jnp.bfloat16) for w in parts], axis=-1),
                key_tile(slab, 1, i, h), preferred_element_type=jnp.float32,
            )

    def attend_tile(p, t):
        tile = p * TD + t
        for h in range(nh):
            if carry is None:
                mbuf[h] = jnp.full(mbuf.shape[1:], -1e30, jnp.float32)
            else:
                mbuf[h] = carry[0][tile, h]
        for group, slab in enumerate(slabs(p)):
            for h in range(nh):
                score(p, t, group, slab, h)
        for h in range(nh):
            top = jnp.max(mbuf[h], axis=-1, keepdims=True)
            mbuf[h] = jnp.broadcast_to(top, (ROWS, 128))
            if carry is None:
                lbuf[h] = jnp.zeros(lbuf.shape[1:], jnp.float32)
                abuf[h] = jnp.zeros(abuf.shape[1:], jnp.float32)
            else:
                scale = jnp.exp2(carry[0][tile, h] - mbuf[h])
                lbuf[h] = carry[1][tile, h] * scale
                abuf[h] = carry[2][tile, h] * scale
        for group, slab in enumerate(slabs(p)):
            for h in range(nh):
                weigh(p, t, group, slab, h)
        for h in range(nh):
            if part == "first":
                outs[0][tile, h] = mbuf[h]
                outs[1][tile, h] = lbuf[h]
                outs[2][tile, h] = abuf[h]
            else:
                total = jnp.sum(lbuf[h], axis=-1, keepdims=True)
                result = (abuf[h] / total).astype(jnp.bfloat16)
                for u in range(4):
                    outs[0][p * 4 + u, t, :, lanes(h)] = result[u * LOC : (u + 1) * LOC]

    for p in range(2):

        @pl.loop(0, TD)
        def _(t):
            attend_tile(p, t)


def attend(part, live, arrays, carry=()):
    width = arrays[0].shape[-1]
    nh = width // HD
    whole = pl.BlockSpec(memory_space=pltpu.VMEM)
    if part == "first":
        shapes = [jax.ShapeDtypeStruct((2 * TD, nh, ROWS, 128), jnp.float32)] * 3
    else:
        shapes = [jax.ShapeDtypeStruct((8, TD, LOC, width), jnp.bfloat16)]
    return pl.pallas_call(
        functools.partial(attend_kernel, part, nh),
        in_specs=[pl.BlockSpec(memory_space=pltpu.SMEM)]
        + [whole] * (len(arrays) + len(carry)),
        out_specs=[whole] * len(shapes),
        out_shape=shapes,
        scratch_shapes=[
            pltpu.VMEM((nh, SLABS[part], ROWS, TD * KEYS), jnp.float32),
            pltpu.VMEM((nh, ROWS, 128), jnp.float32),
            pltpu.VMEM((nh, ROWS, HD), jnp.float32),
            pltpu.VMEM((nh, ROWS, 128), jnp.float32),
        ],
        compiler_params=pltpu.CompilerParams(vmem_limit_bytes=32 << 20),
    )(live, *arrays, *carry)


def unpack_kernel(ref, out_ref):
    width = ref.shape[-1]
    for chip in range(ref.shape[0]):
        out_ref[:, :, chip * width : (chip + 1) * width] = ref[chip]


def unpack(block):
    width = block.shape[-1]
    return pl.pallas_call(
        unpack_kernel,
        grid=(8 // AT_ONCE,),
        in_specs=[pl.BlockSpec((AT_ONCE, TD, LOC, width), lambda i: (i, 0, 0, 0))],
        out_specs=pl.BlockSpec((TD, LOC, AT_ONCE * width), lambda i: (0, 0, i)),
        out_shape=jax.ShapeDtypeStruct((TD, LOC, 24 * HD), jnp.bfloat16),
        name="unpack",
    )(block)


def compute(query_proj, key_proj, value_proj, query_gain, key_gain, neighbours, tile_counts):
    slab = lax.axis_index("ylo")
    column = lax.axis_index("z") * SIZES[3] + lax.axis_index("x")
    table = jnp.concatenate([neighbours, tile_counts[:, None]], axis=1)
    other = lax.ppermute(table, AXES, SWAP_SLAB)
    table = jnp.where(slab == 0, jnp.stack([table, other]), jnp.stack([other, table]))
    table = table.reshape(2 * TD, NB + 1)
    first_tile = (2 * column - 1) * TD + TD * (jnp.arange(2 * TD, dtype=jnp.int32) // TD)
    local = table[:, :NB] - first_tile[:, None]
    place = jnp.arange(NB, dtype=jnp.int32)
    counted = place[None, :] < table[:, NB:]
    match = (local[:, None, :] == place[None, :, None]) & counted[:, None, :]
    live = jnp.any(match, axis=2).astype(jnp.int32)

    block = pack((key_proj, key_gain), (value_proj, None))
    own = lax.all_to_all(block, RING, 0, 0, tiled=True)
    block = pack((query_proj, query_gain))
    query = lax.all_to_all(block, RING, 0, 0, tiled=True)
    prev_own = lax.ppermute(own[4:], AXES, FORWARD)
    next_own = lax.ppermute(own[:4], AXES, BACKWARD)
    mate = lax.ppermute(own, AXES, SWAP_CORE)
    prev_mate = lax.ppermute(prev_own, AXES, SWAP_CORE)
    next_mate = lax.ppermute(next_own, AXES, SWAP_CORE)
    carry = attend("first", live, [query, own, mate])
    halo = [prev_own, prev_mate, next_own, next_mate]
    (done,) = attend("last", live, [query, *halo], carry)
    done = lax.all_to_all(done, RING, 0, 0, tiled=True)
    return unpack(done)


def solution(mesh):
    split = Mesh(mesh.devices.reshape(SIZES), AXES)
    blk, uly = ("z", "x", "ylo"), ("yhi", "core")
    rows = P(blk, uly, None)
    in_specs = (rows, rows, rows, P(), P(), P(blk, None), P(blk))
    return jax.shard_map(compute, mesh=split, in_specs=in_specs, out_specs=rows, check_vma=False)
```
